32 devices in a mesh: gx: 8 (over z, y), gy: 4 (over x, core).
Axes of the slice: x: 2, y: 2, z: 4, core: 2. Of those that a mesh axis runs over, the one named last changes fastest.
Arguments:
- covariance: bfloat16 [4, 32, 32, 4096], P(None, 'gx', 'gy'), may hold values from -8 to 8, as said below
- pilot_ids: int32 [4, 32, 32], P(None, 'gx', 'gy'), may hold values from 0 to 15
- targets: float32 [2, 4, 32, 32], P(None, None, 'gx', 'gy'), may hold values from -6 to 6
- encoder_beam_weight: bfloat16 [64, 512], replicated, may hold values from -1 to 1
- norm_gain: float32 [512], replicated, may hold values from 0.5 to 1.5
- pilot_table: float32 [16, 512], replicated, may hold values from -3 to 3
- pair_weight: bfloat16 [512, 1024], replicated, may hold values from -0.25 to 0.25
- edge_bias: float32 [512], replicated, may hold values from -3 to 3
- node_weight: bfloat16 [1024, 512], replicated, may hold values from -0.1875 to 0.1875
- node_bias: float32 [512], replicated, may hold values from -3 to 3
- update_weight: bfloat16 [512, 512], replicated, may hold values from -0.25 to 0.25
- readout_weight: bfloat16 [2, 512], replicated, may hold values from -0.25 to 0.25
Outputs:
- estimates: float32 [2, 4, 32, 32], P(None, None, 'gx', 'gy')
- grad_pair_weight: float32 [512, 1024], P('gx')
- grad_node_weight: float32 [1024, 512], P('gx')
- grad_update_weight: float32 [512, 512], replicated
- grad_beam_weights: float32 [64, 512], replicated
- grad_edge_bias: float32 [512], replicated
- grad_node_bias: float32 [512], replicated
- grad_norm_gain: float32 [512], replicated
- grad_pilot_table: float32 [16, 512], replicated
- grad_readout_weight: float32 [2, 512], replicated
- point_gradient: float32 [4, 32, 32, 512], P(None, 'gx', 'gy')
The draws below stay inside these ranges and needn't reach their ends.
Inputs may be any that keep to these rules, and one draw needn't show every extreme that they name: `covariance`: each access point's matrix, read as 64 x 64 row by row, is symmetric.
All inputs are finite; a program needn't handle non-finite values.
Results may differ from the reference program's by a relative error of at most 0.0095.
Values may be sent and summed in bfloat16 or wider, within the bound.
A program may use at most 64 MiB of HBM per device.

```python
import math
import jax
import jax.numpy as jnp
from jax import lax

ANTENNA_COUNT = 64
POINT_FEATURES = 512
NPIL = 16
CHANNEL_DRAWS = 4
ROUNDS = 3
GRID_ROW_COUNT = 32
GRID_COLUMNS = 32
LINK_ROWS = 8


def draw_covariance(key, part):
    grid_extent = (CHANNEL_DRAWS, GRID_ROW_COUNT, GRID_COLUMNS, ANTENNA_COUNT, ANTENNA_COUNT)
    pieces = jax.random.normal(key, grid_extent, jnp.float32)
    symmetric_matrix = jnp.clip((pieces + jnp.swapaxes(pieces, -1, -2)) * 0.7071, -8.0, 8.0)
    return symmetric_matrix.reshape(CHANNEL_DRAWS, GRID_ROW_COUNT, GRID_COLUMNS, ANTENNA_COUNT * ANTENNA_COUNT).astype(jnp.bfloat16)


def draw_encoder_beam_weight(key, part):
    entry_key, key_column = jax.random.split(key)
    column_scaling = jnp.exp(jax.random.uniform(key_column, (1, POINT_FEATURES), jnp.float32, math.log(0.3), math.log(3.0)))
    matrix_entries = jax.random.normal(entry_key, (ANTENNA_COUNT, POINT_FEATURES), jnp.float32)
    return jnp.clip(matrix_entries * column_scaling / math.sqrt(ANTENNA_COUNT), -1.0, 1.0).astype(jnp.bfloat16)


def touch_ends(values, rng, low, largest):
    spot = [jax.random.randint(jax.random.fold_in(rng, axis), (), 0, length) for axis, length in enumerate(values.shape)]
    main_axis = values.shape.index(max(values.shape))
    beside = spot[:main_axis] + [(spot[main_axis] + 1) % values.shape[main_axis]] + spot[main_axis + 1:]
    return values.at[tuple(spot)].set(low).at[tuple(beside)].set(largest)


def block_scale(stream_key, extent, cuts, low, top_value):
    gain, own = 1.0, jax.random.fold_in(stream_key, 6)
    for position, parts in cuts:
        draws = jnp.exp(jax.random.uniform(jax.random.fold_in(own, position), (parts,), jnp.float32, low / len(cuts), top_value / len(cuts)))
        gain = gain * jnp.repeat(draws, extent[position] // parts).reshape([-1 if axis == position else 1 for axis in range(len(extent))])
    return gain


def gaussian(own_key, extent, width, bound, cuts=(), kind=jnp.bfloat16):
    result = jax.random.normal(own_key, extent, jnp.float32) * width
    if len(cuts) > 0:
        result = block_scale(own_key, extent, cuts, -0.22, 0.18) * result
    return jnp.clip(result, min=-bound, max=bound).astype(kind)


def setup_inputs(seed: int = 0) -> dict:
    key_of = jax.random.split(jax.random.key(seed), 13)
    covariance = draw_covariance(jax.random.fold_in(key_of[12], 71), 0)
    pilot_ids = touch_ends(jax.random.randint(key_of[1], (CHANNEL_DRAWS, GRID_ROW_COUNT, GRID_COLUMNS), 0, NPIL), jax.random.fold_in(key_of[1], 1), 0, NPIL - 1).astype(jnp.int32)
    targets = gaussian(key_of[2], (2, CHANNEL_DRAWS, GRID_ROW_COUNT, GRID_COLUMNS), 1.0, 6.0, ((2, 8), (3, 4)), jnp.float32)
    encoder_beam_weight = draw_encoder_beam_weight(jax.random.fold_in(key_of[12], 71), 0)
    norm_gain = jnp.clip(1.0 + 0.1 * jax.random.normal(key_of[4], (POINT_FEATURES,), jnp.float32), 0.5, 1.5)
    pilot_table = gaussian(key_of[5], (NPIL, POINT_FEATURES), 0.5, 3.0, (), jnp.float32)
    pair_weight = gaussian(key_of[6], (POINT_FEATURES, 2 * POINT_FEATURES), POINT_FEATURES ** -0.5, 0.25)
    edge_bias = gaussian(key_of[7], (POINT_FEATURES,), 0.5, 3.0, (), jnp.float32)
    node_weight = gaussian(key_of[8], (2 * POINT_FEATURES, POINT_FEATURES), (2 * POINT_FEATURES) ** -0.5, 0.1875)
    node_bias = gaussian(key_of[9], (POINT_FEATURES,), 0.5, 3.0, (), jnp.float32)
    update_weight = gaussian(key_of[10], (POINT_FEATURES, POINT_FEATURES), POINT_FEATURES ** -0.5, 0.25)
    readout_weight = gaussian(key_of[11], (2, POINT_FEATURES), POINT_FEATURES ** -0.5, 0.25)
    return {"covariance": covariance, "pilot_ids": pilot_ids, "targets": targets, "encoder_beam_weight": encoder_beam_weight, "norm_gain": norm_gain, "pilot_table": pilot_table, "pair_weight": pair_weight, "edge_bias": edge_bias, "node_weight": node_weight, "node_bias": node_bias, "update_weight": update_weight, "readout_weight": readout_weight}


EPSILON = 1e-06
GRID_STEPS = [(-1, -1), (-1, 0), (-1, 1), (0, -1), (0, 1), (1, -1), (1, 0), (1, 1)]
HIGHEST = lax.Precision.HIGHEST

def silu_slope(values):
    sigmoid = jax.nn.sigmoid(values)
    return sigmoid * (1.0 + values * (1.0 - sigmoid))

def contract_rows(left_rows, right_rows):
    return lax.dot_general(left_rows, right_rows, (((0,), (0,)), ((), ())), preferred_element_type=jnp.float32)

def times_transpose(left_rows, right_cols):
    return lax.dot_general(left_rows, right_cols, (((1,), (1,)), ((), ())), preferred_element_type=jnp.float32)

def moved(field, row_step, col_step):
    row_pad = abs(row_step)
    col_pad = abs(col_step)
    padded = jnp.pad(field, ((0, 0), (row_pad, row_pad), (col_pad, col_pad), (0, 0)))
    return padded[:, row_pad + row_step:row_pad + row_step + GRID_ROW_COUNT, col_pad + col_step:col_pad + col_step + GRID_COLUMNS]

def inside_mask(row_step, col_step):
    rows_here = lax.broadcasted_iota(jnp.int32, (GRID_ROW_COUNT, GRID_COLUMNS), 0) + row_step
    cols_here = lax.broadcasted_iota(jnp.int32, (GRID_ROW_COUNT, GRID_COLUMNS), 1) + col_step
    inside = (rows_here >= 0) & (rows_here < GRID_ROW_COUNT) & (cols_here >= 0) & (cols_here < GRID_COLUMNS)
    return inside.astype(jnp.float32)[None, :, :, None]

def reference(covariance, pilot_ids, targets, encoder_beam_weight, norm_gain, pilot_table, pair_weight, edge_bias, node_weight, node_bias, update_weight, readout_weight):
    points = CHANNEL_DRAWS * GRID_ROW_COUNT * GRID_COLUMNS
    steps_all = GRID_STEPS + [(LINK_ROWS, 0), (-LINK_ROWS, 0)]
    masks = [inside_mask(row_step, col_step) for row_step, col_step in steps_all]
    degree = masks[0]
    for another in masks[1:]:
        degree = degree + another
    beams = encoder_beam_weight.astype(jnp.float32)
    block_list = covariance.reshape(CHANNEL_DRAWS * GRID_ROW_COUNT, GRID_COLUMNS * ANTENNA_COUNT, ANTENNA_COUNT)

    def block_power(covariance_block):
        projected_beams = jnp.dot(covariance_block, encoder_beam_weight, preferred_element_type=jnp.float32).reshape(GRID_COLUMNS, ANTENNA_COUNT, POINT_FEATURES)
        return lax.optimization_barrier(jnp.sum(projected_beams * beams[None], axis=1))
    powers = lax.map(block_power, block_list).reshape(CHANNEL_DRAWS, GRID_ROW_COUNT, GRID_COLUMNS, POINT_FEATURES)
    inverse = lax.rsqrt(lax.optimization_barrier(jnp.mean(powers * powers, axis=-1, keepdims=True)) + EPSILON)
    normed = powers * inverse
    onehot = (pilot_ids.reshape(points, 1) == jnp.arange(NPIL, dtype=jnp.int32)[None, :]).astype(jnp.float32)
    looked = lax.dot_general(onehot, pilot_table, (((1,), (0,)), ((), ())), precision=HIGHEST, preferred_element_type=jnp.float32)
    hidden = normed * norm_gain + looked.reshape(CHANNEL_DRAWS, GRID_ROW_COUNT, GRID_COLUMNS, POINT_FEATURES)
    records = []
    for round_index in range(ROUNDS):
        flat_state = hidden.astype(jnp.bfloat16).reshape(points, POINT_FEATURES)
        projected_beams = jnp.dot(flat_state, pair_weight, preferred_element_type=jnp.float32).reshape(CHANNEL_DRAWS, GRID_ROW_COUNT, GRID_COLUMNS, 2 * POINT_FEATURES)
        query_part = projected_beams[..., :POINT_FEATURES].astype(jnp.bfloat16)
        key_part = projected_beams[..., POINT_FEATURES:].astype(jnp.bfloat16)
        query_wide = query_part.astype(jnp.float32)
        edge_total = jnp.zeros((CHANNEL_DRAWS, GRID_ROW_COUNT, GRID_COLUMNS, POINT_FEATURES), jnp.float32)
        for inside, (row_step, col_step) in zip(masks, steps_all):
            other_key = moved(key_part, row_step, col_step).astype(jnp.float32)
            edge_total = edge_total + inside * jax.nn.silu(query_wide + other_key + edge_bias)
        flat_message = (edge_total / degree).astype(jnp.bfloat16).reshape(points, POINT_FEATURES)
        before = jnp.dot(flat_state, node_weight[:POINT_FEATURES], preferred_element_type=jnp.float32) + jnp.dot(flat_message, node_weight[POINT_FEATURES:], preferred_element_type=jnp.float32) + node_bias
        update = jax.nn.silu(before).astype(jnp.bfloat16)
        hidden = hidden + jnp.dot(update, update_weight, preferred_element_type=jnp.float32).reshape(CHANNEL_DRAWS, GRID_ROW_COUNT, GRID_COLUMNS, POINT_FEATURES)
        records.append((flat_state, query_part, key_part, flat_message, before, update))
    final_state = hidden.astype(jnp.bfloat16).reshape(points, POINT_FEATURES)
    estimates = times_transpose(readout_weight, final_state)
    residual_slope = (estimates - targets.reshape(2, points)) * (2.0 / math.sqrt(points))
    grad_readout = lax.dot_general(residual_slope, final_state.astype(jnp.float32), (((1,), (0,)), ((), ())), precision=HIGHEST, preferred_element_type=jnp.float32)
    readout_wide = readout_weight.astype(jnp.float32)
    grad_hidden = residual_slope[0][:, None] * readout_wide[0][None, :] + residual_slope[1][:, None] * readout_wide[1][None, :]
    grad_update = jnp.zeros((POINT_FEATURES, POINT_FEATURES), jnp.float32)
    grad_node = jnp.zeros((2 * POINT_FEATURES, POINT_FEATURES), jnp.float32)
    grad_pair = jnp.zeros((POINT_FEATURES, 2 * POINT_FEATURES), jnp.float32)
    grad_node_bias = jnp.zeros((POINT_FEATURES,), jnp.float32)
    grad_edge_bias = jnp.zeros((POINT_FEATURES,), jnp.float32)
    for flat_state, query_part, key_part, flat_message, before, update in reversed(records):
        down_rows = grad_hidden.astype(jnp.bfloat16)
        grad_update = grad_update + contract_rows(update, down_rows)
        grad_before = times_transpose(down_rows, update_weight) * silu_slope(before)
        grad_node_bias = grad_node_bias + lax.optimization_barrier(jnp.sum(grad_before, axis=0))
        lower_rows = grad_before.astype(jnp.bfloat16)
        grad_node = grad_node + contract_rows(jnp.concatenate([flat_state, flat_message], axis=1), lower_rows)
        grad_inputs = times_transpose(lower_rows, node_weight)
        sending = (grad_inputs[:, POINT_FEATURES:].reshape(CHANNEL_DRAWS, GRID_ROW_COUNT, GRID_COLUMNS, POINT_FEATURES) / degree).astype(jnp.bfloat16)
        sending_wide = sending.astype(jnp.float32)
        query_wide = query_part.astype(jnp.float32)
        key_wide = key_part.astype(jnp.float32)
        grad_query = jnp.zeros((CHANNEL_DRAWS, GRID_ROW_COUNT, GRID_COLUMNS, POINT_FEATURES), jnp.float32)
        grad_key = jnp.zeros((CHANNEL_DRAWS, GRID_ROW_COUNT, GRID_COLUMNS, POINT_FEATURES), jnp.float32)
        for inside, (row_step, col_step) in zip(masks, steps_all):
            other_key = moved(key_part, row_step, col_step).astype(jnp.float32)
            grad_query = grad_query + inside * sending_wide * silu_slope(query_wide + other_key + edge_bias)
            other_query = moved(query_part, row_step, col_step).astype(jnp.float32)
            other_sending = moved(sending, row_step, col_step).astype(jnp.float32)
            grad_key = grad_key + inside * other_sending * silu_slope(other_query + key_wide + edge_bias)
        grad_edge_bias = grad_edge_bias + lax.optimization_barrier(jnp.sum(grad_query, axis=(0, 1, 2)))
        pair_rows = jnp.concatenate([grad_query, grad_key], axis=-1).astype(jnp.bfloat16).reshape(points, 2 * POINT_FEATURES)
        grad_pair = grad_pair + contract_rows(flat_state, pair_rows)
        grad_hidden = grad_hidden + grad_inputs[:, :POINT_FEATURES] + times_transpose(pair_rows, pair_weight)
    grad_zero = grad_hidden.reshape(CHANNEL_DRAWS, GRID_ROW_COUNT, GRID_COLUMNS, POINT_FEATURES)
    point_gradient = grad_zero * math.sqrt(points)
    grad_gain = lax.optimization_barrier(jnp.sum(grad_zero * normed, axis=(0, 1, 2)))
    grad_table = lax.dot_general(onehot, grad_hidden, (((0,), (0,)), ((), ())), precision=HIGHEST, preferred_element_type=jnp.float32)
    scaled = grad_zero * norm_gain
    power_gradient = inverse * (scaled - normed * lax.optimization_barrier(jnp.mean(scaled * normed, axis=-1, keepdims=True)))

    def beam_update_step(running, inputs):
        covariance_block, weight_rows = inputs
        projected_beams = jnp.dot(covariance_block, encoder_beam_weight, preferred_element_type=jnp.float32).reshape(GRID_COLUMNS, ANTENNA_COUNT, POINT_FEATURES)
        return (running + lax.optimization_barrier(jnp.sum(projected_beams * weight_rows[:, None, :], axis=0)), None)
    beam_gradient, ignored_value = lax.scan(beam_update_step, jnp.zeros((ANTENNA_COUNT, POINT_FEATURES), jnp.float32), (block_list, power_gradient.reshape(CHANNEL_DRAWS * GRID_ROW_COUNT, GRID_COLUMNS, POINT_FEATURES)))
    beam_gradient = 2.0 * beam_gradient
    return (estimates.reshape(2, CHANNEL_DRAWS, GRID_ROW_COUNT, GRID_COLUMNS), grad_pair, grad_node, grad_update, beam_gradient, grad_edge_bias, grad_node_bias, grad_gain, grad_table, grad_readout, point_gradient)
```

```python
import math

import jax
import jax.numpy as jnp
from jax import lax
from jax.sharding import PartitionSpec as P

ROUNDS = 3


EPSILON = 1e-06
GRID_STEPS = [(-1, -1), (-1, 0), (-1, 1), (0, -1), (0, 1), (1, -1), (1, 0), (1, 1)]
HIGHEST = lax.Precision.HIGHEST


def with_halo(cells, sides, width):
    for axis, dim in sides:
        count = lax.axis_size(axis)
        ends = count - 1
        head = lax.slice_in_dim(cells, 0, width, axis=dim)
        tail = lax.slice_in_dim(cells, cells.shape[dim] - width, cells.shape[dim], axis=dim)
        cells = jnp.concatenate(
            [
                lax.ppermute(tail, axis, [(i, (i + 1) % count) for i in range(ends)]),
                cells,
                lax.ppermute(head, axis, [((i + 1) % count, i) for i in range(ends)]),
            ],
            axis=dim,
        )
    return cells


def from_behind(value, axis, steps):
    count = lax.axis_size(axis)
    leading, last = (max(0, -steps), min(count, count - steps))
    return lax.ppermute(value, axis, [(source, source + steps) for source in range(leading, last)])


def silu_slope(values):
    sigmoid = jax.nn.sigmoid(values)
    return sigmoid * (1.0 + values * (1.0 - sigmoid))


def contract_rows(left_rows, right_rows):
    return lax.dot_general(
        left_rows, right_rows, (((0,), (0,)), ((), ())), preferred_element_type=jnp.float32
    )


def times_transpose(left_rows, right_cols):
    return lax.dot_general(
        left_rows, right_cols, (((1,), (1,)), ((), ())), preferred_element_type=jnp.float32
    )


def arrange(padded, distant, height, width):
    nearby = [
        padded[:, 1 + row_step : 1 + row_step + height, 1 + col_step : 1 + col_step + width]
        for row_step, col_step in GRID_STEPS
    ]
    return nearby + list(distant)


def validity(height, width, span_rows):
    row_first = lax.axis_index("gx") * height
    col_first = lax.axis_index("gy") * width
    total_rows = height * lax.axis_size("gx")
    total_cols = width * lax.axis_size("gy")
    rows_here = row_first + lax.broadcasted_iota(jnp.int32, (height, width), 0)
    cols_here = col_first + lax.broadcasted_iota(jnp.int32, (height, width), 1)
    masks = []
    for row_step, col_step in GRID_STEPS + [(span_rows, 0), (-span_rows, 0)]:
        inside = (
            (rows_here + row_step >= 0)
            & (rows_here + row_step < total_rows)
            & (cols_here + col_step >= 0)
            & (cols_here + col_step < total_cols)
        )
        masks.append(inside.astype(jnp.float32)[None, :, :, None])
    return masks


def fetch_forward(field, span):
    padded = with_halo(field, (("gx", 1), ("gy", 2)), 1)
    distant = [from_behind(field, "gx", moved_by) for moved_by in (-span, span)]
    return (padded, distant)


def fetch_pair(field, span):
    padded = with_halo(field, (("gx", 1), ("gy", 2)), 1)
    distant = [from_behind(field, "gx", moved_by) for moved_by in (-span, span)]
    return (padded, distant)


def on_device(
    covariance,
    pilot_ids,
    targets,
    encoder_beam_weight,
    norm_gain,
    pilot_table,
    pair_weight,
    edge_bias,
    node_weight,
    node_bias,
    update_weight,
    readout_weight,
):
    samples, height, width = (covariance.shape[0], covariance.shape[1], covariance.shape[2])
    antennas = encoder_beam_weight.shape[0]
    features = encoder_beam_weight.shape[1]
    pilots = pilot_table.shape[0]
    span = lax.axis_size("gx") // 4
    span_rows = span * height
    points = samples * height * width
    total_points = points * lax.axis_size("gx") * lax.axis_size("gy")
    masks = validity(height, width, span_rows)
    degree = masks[0]
    for another in masks[1:]:
        degree = degree + another
    beams = encoder_beam_weight.astype(jnp.float32)
    cov_flat = covariance.reshape(points, antennas * antennas)
    outer = (beams[:, None, :] * beams[None, :, :]).reshape(antennas * antennas, features)
    outer_hi = outer.astype(jnp.bfloat16)
    outer_lo = (outer - outer_hi.astype(jnp.float32)).astype(jnp.bfloat16)
    powers = (
        jnp.dot(cov_flat, outer_hi, preferred_element_type=jnp.float32)
        + jnp.dot(cov_flat, outer_lo, preferred_element_type=jnp.float32)
    ).reshape(samples, height, width, features)
    inverse = lax.rsqrt(jnp.mean(powers * powers, axis=-1, keepdims=True) + EPSILON)
    normed = powers * inverse
    onehot = (pilot_ids.reshape(points, 1) == jnp.arange(pilots, dtype=jnp.int32)[None, :]).astype(
        jnp.float32
    )
    looked = lax.dot_general(
        onehot,
        pilot_table,
        (((1,), (0,)), ((), ())),
        precision=HIGHEST,
        preferred_element_type=jnp.float32,
    )
    hidden = normed * norm_gain + looked.reshape(samples, height, width, features)
    saved = []
    for round_index in range(ROUNDS):
        flat_hidden = hidden.astype(jnp.bfloat16).reshape(points, features)
        pair_proj = jnp.dot(flat_hidden, pair_weight, preferred_element_type=jnp.float32).reshape(
            samples, height, width, 2 * features
        )
        query_part = pair_proj[..., :features].astype(jnp.bfloat16)
        key_part = pair_proj[..., features:].astype(jnp.bfloat16)
        padded, distant = fetch_forward(key_part, span)
        key_near = arrange(padded, distant, height, width)
        query_kept = None
        query_wide = query_part.astype(jnp.float32)
        edge_total = jnp.zeros((samples, height, width, features), jnp.float32)
        for inside, neighbour in zip(masks, key_near):
            edge_total = edge_total + inside * jax.nn.silu(
                query_wide + neighbour.astype(jnp.float32) + edge_bias
            )
        flat_message = (edge_total / degree).astype(jnp.bfloat16).reshape(points, features)
        before = (
            jnp.dot(flat_hidden, node_weight[:features], preferred_element_type=jnp.float32)
            + jnp.dot(flat_message, node_weight[features:], preferred_element_type=jnp.float32)
            + node_bias
        )
        update = jax.nn.silu(before).astype(jnp.bfloat16)
        hidden = hidden + jnp.dot(
            update, update_weight, preferred_element_type=jnp.float32
        ).reshape(samples, height, width, features)
        saved.append(
            (flat_hidden, query_part, key_part, key_near, query_kept, flat_message, before, update)
        )
    final_flat = hidden.astype(jnp.bfloat16).reshape(points, features)
    estimates = times_transpose(readout_weight, final_flat)
    residual_slope = (estimates - targets.reshape(2, points)) * (2.0 / math.sqrt(total_points))
    grad_readout = lax.dot_general(
        residual_slope,
        final_flat.astype(jnp.float32),
        (((1,), (0,)), ((), ())),
        precision=HIGHEST,
        preferred_element_type=jnp.float32,
    )
    readout_wide = readout_weight.astype(jnp.float32)
    grad_hidden = (
        residual_slope[0][:, None] * readout_wide[0][None, :]
        + residual_slope[1][:, None] * readout_wide[1][None, :]
    )
    grad_update = jnp.zeros((features, features), jnp.float32)
    grad_node_bias = jnp.zeros((features,), jnp.float32)
    grad_edge_bias = jnp.zeros((features,), jnp.float32)
    state_list, pair_list, input_list, lower_list = ([], [], [], [])
    for (
        flat_hidden,
        query_part,
        key_part,
        key_near,
        query_kept,
        flat_message,
        before,
        update,
    ) in reversed(saved):
        down_rows = grad_hidden.astype(jnp.bfloat16)
        grad_update = grad_update + contract_rows(update, down_rows)
        grad_before = times_transpose(down_rows, update_weight) * silu_slope(before)
        grad_node_bias = grad_node_bias + jnp.sum(grad_before, axis=0)
        lower_rows = grad_before.astype(jnp.bfloat16)
        grad_inputs = times_transpose(lower_rows, node_weight)
        sending = (
            grad_inputs[:, features:].reshape(samples, height, width, features) / degree
        ).astype(jnp.bfloat16)
        stacked = jnp.concatenate([query_part, sending], axis=-1)
        padded_pair, distant_pair = fetch_pair(stacked, span)
        pair_near = arrange(padded_pair, distant_pair, height, width)
        query_near = [piece_pair[..., :features] for piece_pair in pair_near]
        sending_near = [piece_pair[..., features:] for piece_pair in pair_near]
        sending_wide = sending.astype(jnp.float32)
        query_wide = query_part.astype(jnp.float32)
        key_wide = key_part.astype(jnp.float32)
        grad_query = jnp.zeros((samples, height, width, features), jnp.float32)
        grad_key = jnp.zeros((samples, height, width, features), jnp.float32)
        for inside, key_other, query_other, sending_other in zip(
            masks, key_near, query_near, sending_near
        ):
            grad_query = grad_query + inside * sending_wide * silu_slope(
                query_wide + key_other.astype(jnp.float32) + edge_bias
            )
            grad_key = grad_key + inside * sending_other.astype(jnp.float32) * silu_slope(
                query_other.astype(jnp.float32) + key_wide + edge_bias
            )
        grad_edge_bias = grad_edge_bias + jnp.sum(grad_query, axis=(0, 1, 2))
        pair_rows = (
            jnp.concatenate([grad_query, grad_key], axis=-1)
            .astype(jnp.bfloat16)
            .reshape(points, 2 * features)
        )
        grad_hidden = (
            grad_hidden + grad_inputs[:, :features] + times_transpose(pair_rows, pair_weight)
        )
        state_list.append(flat_hidden)
        pair_list.append(pair_rows)
        input_list.append(jnp.concatenate([flat_hidden, flat_message], axis=1))
        lower_list.append(lower_rows)
    grad_zero = grad_hidden.reshape(samples, height, width, features)
    point_gradient = grad_zero * math.sqrt(total_points)
    grad_gain = jnp.sum(grad_zero * normed, axis=(0, 1, 2))
    grad_table = lax.dot_general(
        onehot,
        grad_hidden,
        (((0,), (0,)), ((), ())),
        precision=HIGHEST,
        preferred_element_type=jnp.float32,
    )
    scaled = grad_zero * norm_gain
    power_gradient = inverse * (scaled - normed * jnp.mean(scaled * normed, axis=-1, keepdims=True))

    power_rows = power_gradient.reshape(points, features)
    power_hi = power_rows.astype(jnp.bfloat16)
    power_lo = (power_rows - power_hi.astype(jnp.float32)).astype(jnp.bfloat16)
    spread = contract_rows(cov_flat, power_hi) + contract_rows(cov_flat, power_lo)
    beam_gradient = jnp.sum(
        spread.reshape(antennas, antennas, features) * beams[None, :, :], axis=1
    )
    beam_gradient = 2.0 * beam_gradient
    small_sums = lax.psum(
        (
            grad_update,
            beam_gradient,
            grad_edge_bias,
            grad_node_bias,
            grad_gain,
            grad_table,
            grad_readout,
        ),
        ("gx", "gy"),
    )
    rows_state = jnp.concatenate(state_list, axis=0)
    rows_pair = jnp.concatenate(pair_list, axis=0)
    rows_input = jnp.concatenate(input_list, axis=0)
    rows_lower = jnp.concatenate(lower_list, axis=0)
    sliced = rows_state
    pair_part = lax.psum_scatter(
        contract_rows(sliced, rows_pair), "gx", scatter_dimension=0, tiled=True
    )
    sliced = rows_input
    node_part = lax.psum_scatter(
        contract_rows(sliced, rows_lower), "gx", scatter_dimension=0, tiled=True
    )
    grad_pair_weight, grad_node_weight = lax.psum((pair_part, node_part), "gy")
    return (
        estimates.reshape(2, samples, height, width),
        grad_pair_weight,
        grad_node_weight,
        small_sums[0],
        small_sums[1],
        small_sums[2],
        small_sums[3],
        small_sums[4],
        small_sums[5],
        small_sums[6],
        point_gradient,
    )


def solution(mesh):
    in_specs = (
        P(None, "gx", "gy", None),
        P(None, "gx", "gy"),
        P(None, None, "gx", "gy"),
        P(),
        P(),
        P(),
        P(),
        P(),
        P(),
        P(),
        P(),
        P(),
    )
    out_specs = (
        P(None, None, "gx", "gy"),
        P("gx", None),
        P("gx", None),
        P(),
        P(),
        P(),
        P(),
        P(),
        P(),
        P(),
        P(None, "gx", "gy", None),
    )
    return jax.shard_map(
        on_device, mesh=mesh, in_specs=in_specs, out_specs=out_specs, check_vma=False
    )
```

```python
import math

import jax
import jax.numpy as jnp
from jax import lax
from jax.sharding import PartitionSpec as P

ROUNDS = 3


EPSILON = 1e-06
GRID_STEPS = [(-1, -1), (-1, 0), (-1, 1), (0, -1), (0, 1), (1, -1), (1, 0), (1, 1)]
HIGHEST = lax.Precision.HIGHEST


def with_halo(cells, sides, width):
    for axis, dim in sides:
        count = lax.axis_size(axis)
        ends = count - 1
        head = lax.slice_in_dim(cells, 0, width, axis=dim)
        tail = lax.slice_in_dim(cells, cells.shape[dim] - width, cells.shape[dim], axis=dim)
        cells = jnp.concatenate(
            [
                lax.ppermute(tail, axis, [(i, (i + 1) % count) for i in range(ends)]),
                cells,
                lax.ppermute(head, axis, [((i + 1) % count, i) for i in range(ends)]),
            ],
            axis=dim,
        )
    return cells


def from_behind(value, axis, steps):
    count = lax.axis_size(axis)
    leading, last = (max(0, -steps), min(count, count - steps))
    return lax.ppermute(value, axis, [(source, source + steps) for source in range(leading, last)])


def exchange(value, axis, flip):
    size = lax.axis_size(axis)
    return lax.ppermute(value, axis, [(i, i ^ flip) for i in range(size)])


def bit_of(axis, flip):
    return (lax.axis_index(axis) // flip) % 2


def flips_of(axis):
    flips = []
    flip = 1
    while flip < lax.axis_size(axis):
        flips.append((axis, flip))
        flip *= 2
    return flips


def halving_sum(buf, names, order):
    for axis, flip in order:
        dim = names.index((axis, flip))
        bit = bit_of(axis, flip)
        keep = lax.dynamic_index_in_dim(buf, bit, axis=dim, keepdims=False)
        send = lax.dynamic_index_in_dim(buf, 1 - bit, axis=dim, keepdims=False)
        buf = keep + exchange(send, axis, flip)
        names = names[:dim] + names[dim + 1 :]
    return buf


def doubling_gather(chunk, order):
    names = []
    for axis, flip in order:
        bit = bit_of(axis, flip)
        got = exchange(chunk, axis, flip)
        low = jnp.where(bit == 0, chunk, got)
        high = jnp.where(bit == 0, got, chunk)
        chunk = jnp.stack([low, high], axis=0)
        names = [(axis, flip)] + names
    return chunk, names


def silu_slope(values):
    sigmoid = jax.nn.sigmoid(values)
    return sigmoid * (1.0 + values * (1.0 - sigmoid))


def contract_rows(left_rows, right_rows):
    return lax.dot_general(
        left_rows, right_rows, (((0,), (0,)), ((), ())), preferred_element_type=jnp.float32
    )


def times_transpose(left_rows, right_cols):
    return lax.dot_general(
        left_rows, right_cols, (((1,), (1,)), ((), ())), preferred_element_type=jnp.float32
    )


def arrange(padded, distant, height, width):
    nearby = [
        padded[:, 1 + row_step : 1 + row_step + height, 1 + col_step : 1 + col_step + width]
        for row_step, col_step in GRID_STEPS
    ]
    return nearby + list(distant)


def validity(height, width, span_rows):
    row_first = lax.axis_index("gx") * height
    col_first = lax.axis_index("gy") * width
    total_rows = height * lax.axis_size("gx")
    total_cols = width * lax.axis_size("gy")
    rows_here = row_first + lax.broadcasted_iota(jnp.int32, (height, width), 0)
    cols_here = col_first + lax.broadcasted_iota(jnp.int32, (height, width), 1)
    masks = []
    for row_step, col_step in GRID_STEPS + [(span_rows, 0), (-span_rows, 0)]:
        inside = (
            (rows_here + row_step >= 0)
            & (rows_here + row_step < total_rows)
            & (cols_here + col_step >= 0)
            & (cols_here + col_step < total_cols)
        )
        masks.append(inside.astype(jnp.float32)[None, :, :, None])
    return masks


def fetch_forward(field, span):
    padded = with_halo(field, (("gx", 1), ("gy", 2)), 1)
    distant = [from_behind(field, "gx", moved_by) for moved_by in (-span, span)]
    return (padded, distant)


def fetch_pair(field, span):
    padded = with_halo(field, (("gx", 1), ("gy", 2)), 1)
    distant = [from_behind(field, "gx", moved_by) for moved_by in (-span, span)]
    return (padded, distant)


def on_device(
    covariance,
    pilot_ids,
    targets,
    encoder_beam_weight,
    norm_gain,
    pilot_table,
    pair_weight,
    edge_bias,
    node_weight,
    node_bias,
    update_weight,
    readout_weight,
):
    samples, height, width = (covariance.shape[0], covariance.shape[1], covariance.shape[2])
    antennas = encoder_beam_weight.shape[0]
    features = encoder_beam_weight.shape[1]
    pilots = pilot_table.shape[0]
    span = lax.axis_size("gx") // 4
    span_rows = span * height
    points = samples * height * width
    total_points = points * lax.axis_size("gx") * lax.axis_size("gy")
    masks = validity(height, width, span_rows)
    degree = masks[0]
    for another in masks[1:]:
        degree = degree + another
    beams = encoder_beam_weight.astype(jnp.float32)
    cov_flat = covariance.reshape(points, antennas * antennas)
    outer = (beams[:, None, :] * beams[None, :, :]).reshape(antennas * antennas, features)
    outer_hi = outer.astype(jnp.bfloat16)
    outer_lo = (outer - outer_hi.astype(jnp.float32)).astype(jnp.bfloat16)
    powers = (
        jnp.dot(cov_flat, outer_hi, preferred_element_type=jnp.float32)
        + jnp.dot(cov_flat, outer_lo, preferred_element_type=jnp.float32)
    ).reshape(samples, height, width, features)
    inverse = lax.rsqrt(jnp.mean(powers * powers, axis=-1, keepdims=True) + EPSILON)
    normed = powers * inverse
    onehot = (pilot_ids.reshape(points, 1) == jnp.arange(pilots, dtype=jnp.int32)[None, :]).astype(
        jnp.float32
    )
    looked = lax.dot_general(
        onehot,
        pilot_table,
        (((1,), (0,)), ((), ())),
        precision=HIGHEST,
        preferred_element_type=jnp.float32,
    )
    hidden = normed * norm_gain + looked.reshape(samples, height, width, features)
    saved = []
    for round_index in range(ROUNDS):
        flat_hidden = hidden.astype(jnp.bfloat16).reshape(points, features)
        pair_proj = jnp.dot(flat_hidden, pair_weight, preferred_element_type=jnp.float32).reshape(
            samples, height, width, 2 * features
        )
        query_part = pair_proj[..., :features].astype(jnp.bfloat16)
        key_part = pair_proj[..., features:].astype(jnp.bfloat16)
        padded, distant = fetch_forward(key_part, span)
        key_near = arrange(padded, distant, height, width)
        query_kept = None
        query_wide = query_part.astype(jnp.float32)
        edge_total = jnp.zeros((samples, height, width, features), jnp.float32)
        for inside, neighbour in zip(masks, key_near):
            edge_total = edge_total + inside * jax.nn.silu(
                query_wide + neighbour.astype(jnp.float32) + edge_bias
            )
        flat_message = (edge_total / degree).astype(jnp.bfloat16).reshape(points, features)
        before = (
            jnp.dot(flat_hidden, node_weight[:features], preferred_element_type=jnp.float32)
            + jnp.dot(flat_message, node_weight[features:], preferred_element_type=jnp.float32)
            + node_bias
        )
        update = jax.nn.silu(before).astype(jnp.bfloat16)
        hidden = hidden + jnp.dot(
            update, update_weight, preferred_element_type=jnp.float32
        ).reshape(samples, height, width, features)
        saved.append(
            (flat_hidden, query_part, key_part, key_near, query_kept, flat_message, before, update)
        )
    final_flat = hidden.astype(jnp.bfloat16).reshape(points, features)
    estimates = times_transpose(readout_weight, final_flat)
    residual_slope = (estimates - targets.reshape(2, points)) * (2.0 / math.sqrt(total_points))
    grad_readout = lax.dot_general(
        residual_slope,
        final_flat.astype(jnp.float32),
        (((1,), (0,)), ((), ())),
        precision=HIGHEST,
        preferred_element_type=jnp.float32,
    )
    readout_wide = readout_weight.astype(jnp.float32)
    grad_hidden = (
        residual_slope[0][:, None] * readout_wide[0][None, :]
        + residual_slope[1][:, None] * readout_wide[1][None, :]
    )
    grad_update = jnp.zeros((features, features), jnp.float32)
    grad_node_bias = jnp.zeros((features,), jnp.float32)
    grad_edge_bias = jnp.zeros((features,), jnp.float32)
    state_list, pair_list, input_list, lower_list = ([], [], [], [])
    for (
        flat_hidden,
        query_part,
        key_part,
        key_near,
        query_kept,
        flat_message,
        before,
        update,
    ) in reversed(saved):
        down_rows = grad_hidden.astype(jnp.bfloat16)
        grad_update = grad_update + contract_rows(update, down_rows)
        grad_before = times_transpose(down_rows, update_weight) * silu_slope(before)
        grad_node_bias = grad_node_bias + jnp.sum(grad_before, axis=0)
        lower_rows = grad_before.astype(jnp.bfloat16)
        grad_inputs = times_transpose(lower_rows, node_weight)
        sending = (
            grad_inputs[:, features:].reshape(samples, height, width, features) / degree
        ).astype(jnp.bfloat16)
        stacked = jnp.concatenate([query_part, sending], axis=-1)
        padded_pair, distant_pair = fetch_pair(stacked, span)
        pair_near = arrange(padded_pair, distant_pair, height, width)
        query_near = [piece_pair[..., :features] for piece_pair in pair_near]
        sending_near = [piece_pair[..., features:] for piece_pair in pair_near]
        sending_wide = sending.astype(jnp.float32)
        query_wide = query_part.astype(jnp.float32)
        key_wide = key_part.astype(jnp.float32)
        grad_query = jnp.zeros((samples, height, width, features), jnp.float32)
        grad_key = jnp.zeros((samples, height, width, features), jnp.float32)
        for inside, key_other, query_other, sending_other in zip(
            masks, key_near, query_near, sending_near
        ):
            grad_query = grad_query + inside * sending_wide * silu_slope(
                query_wide + key_other.astype(jnp.float32) + edge_bias
            )
            grad_key = grad_key + inside * sending_other.astype(jnp.float32) * silu_slope(
                query_other.astype(jnp.float32) + key_wide + edge_bias
            )
        grad_edge_bias = grad_edge_bias + jnp.sum(grad_query, axis=(0, 1, 2))
        pair_rows = (
            jnp.concatenate([grad_query, grad_key], axis=-1)
            .astype(jnp.bfloat16)
            .reshape(points, 2 * features)
        )
        grad_hidden = (
            grad_hidden + grad_inputs[:, :features] + times_transpose(pair_rows, pair_weight)
        )
        state_list.append(flat_hidden)
        pair_list.append(pair_rows)
        input_list.append(jnp.concatenate([flat_hidden, flat_message], axis=1))
        lower_list.append(lower_rows)
    grad_zero = grad_hidden.reshape(samples, height, width, features)
    point_gradient = grad_zero * math.sqrt(total_points)
    grad_gain = jnp.sum(grad_zero * normed, axis=(0, 1, 2))
    grad_table = lax.dot_general(
        onehot,
        grad_hidden,
        (((0,), (0,)), ((), ())),
        precision=HIGHEST,
        preferred_element_type=jnp.float32,
    )
    scaled = grad_zero * norm_gain
    power_gradient = inverse * (scaled - normed * jnp.mean(scaled * normed, axis=-1, keepdims=True))

    power_rows = power_gradient.reshape(points, features)
    power_hi = power_rows.astype(jnp.bfloat16)
    power_lo = (power_rows - power_hi.astype(jnp.float32)).astype(jnp.bfloat16)
    spread = contract_rows(cov_flat, power_hi) + contract_rows(cov_flat, power_lo)
    beam_gradient = jnp.sum(
        spread.reshape(antennas, antennas, features) * beams[None, :, :], axis=1
    )
    rows_state = jnp.concatenate(state_list, axis=0)
    rows_pair = jnp.concatenate(pair_list, axis=0)
    rows_input = jnp.concatenate(input_list, axis=0)
    rows_lower = jnp.concatenate(lower_list, axis=0)
    pair_full = contract_rows(rows_state, rows_pair)
    node_full = contract_rows(rows_input, rows_lower)
    x_flips = flips_of("gx")
    y_flips = flips_of("gy")
    x_count = lax.axis_size("gx")
    y_count = lax.axis_size("gy")
    pieces = x_count * y_count
    replicated = [
        grad_update,
        2.0 * beam_gradient,
        grad_edge_bias,
        grad_node_bias,
        grad_gain,
        grad_table,
        grad_readout,
    ]
    rep_flat = jnp.concatenate([part.reshape(-1) for part in replicated])
    rep_size = rep_flat.shape[0]
    rep_piece = -(-rep_size // pieces)
    rep_flat = jnp.pad(rep_flat, (0, rep_piece * pieces - rep_size))
    buf = jnp.concatenate(
        [
            pair_full.reshape(pieces, -1),
            node_full.reshape(pieces, -1),
            rep_flat.reshape(pieces, rep_piece),
        ],
        axis=1,
    )
    pair_width = pair_full.size // pieces
    node_width = node_full.size // pieces
    msb_x = list(reversed(x_flips))
    msb_y = list(reversed(y_flips))
    names = msb_x + msb_y
    buf = buf.reshape([2] * len(names) + [buf.shape[1]])
    chunk = halving_sum(buf, names, y_flips + x_flips)
    gathered, got_names = doubling_gather(chunk, msb_y)
    gathered = jnp.transpose(
        gathered, [got_names.index(name) for name in msb_y] + [len(got_names)]
    ).reshape(y_count, -1)
    grad_pair_weight = gathered[:, :pair_width].reshape(-1, pair_full.shape[1])
    grad_node_weight = gathered[:, pair_width : pair_width + node_width].reshape(
        -1, node_full.shape[1]
    )
    rep_part = gathered[:, pair_width + node_width :]
    rep_all, rep_names = doubling_gather(rep_part, msb_x)
    rep_all = jnp.transpose(
        rep_all, [rep_names.index(name) for name in msb_x] + [len(rep_names), len(rep_names) + 1]
    ).reshape(-1)
    small_sums = []
    offset = 0
    for part in replicated:
        small_sums.append(rep_all[offset : offset + part.size].reshape(part.shape))
        offset += part.size
    return (
        estimates.reshape(2, samples, height, width),
        grad_pair_weight,
        grad_node_weight,
        small_sums[0],
        small_sums[1],
        small_sums[2],
        small_sums[3],
        small_sums[4],
        small_sums[5],
        small_sums[6],
        point_gradient,
    )


def solution(mesh):
    in_specs = (
        P(None, "gx", "gy", None),
        P(None, "gx", "gy"),
        P(None, None, "gx", "gy"),
        P(),
        P(),
        P(),
        P(),
        P(),
        P(),
        P(),
        P(),
        P(),
    )
    out_specs = (
        P(None, None, "gx", "gy"),
        P("gx", None),
        P("gx", None),
        P(),
        P(),
        P(),
        P(),
        P(),
        P(),
        P(),
        P(None, "gx", "gy", None),
    )
    return jax.shard_map(
        on_device, mesh=mesh, in_specs=in_specs, out_specs=out_specs, check_vma=False
    )
```

```python
import math

import jax
import jax.numpy as jnp
from jax import lax
from jax.sharding import PartitionSpec as P

ROUNDS = 3


EPSILON = 1e-06
GRID_STEPS = [(-1, -1), (-1, 0), (-1, 1), (0, -1), (0, 1), (1, -1), (1, 0), (1, 1)]
HIGHEST = lax.Precision.HIGHEST


def with_halo(cells, sides, width):
    for axis, dim in sides:
        count = lax.axis_size(axis)
        ends = count - 1
        head = lax.slice_in_dim(cells, 0, width, axis=dim)
        tail = lax.slice_in_dim(cells, cells.shape[dim] - width, cells.shape[dim], axis=dim)
        cells = jnp.concatenate(
            [
                lax.ppermute(tail, axis, [(i, (i + 1) % count) for i in range(ends)]),
                cells,
                lax.ppermute(head, axis, [((i + 1) % count, i) for i in range(ends)]),
            ],
            axis=dim,
        )
    return cells


def from_behind(value, axis, steps):
    count = lax.axis_size(axis)
    leading, last = (max(0, -steps), min(count, count - steps))
    return lax.ppermute(value, axis, [(source, source + steps) for source in range(leading, last)])


def exchange(value, axis, flip):
    size = lax.axis_size(axis)
    return lax.ppermute(value, axis, [(i, i ^ flip) for i in range(size)])


def bit_of(axis, flip):
    return (lax.axis_index(axis) // flip) % 2


def flips_of(axis):
    flips = []
    flip = 1
    while flip < lax.axis_size(axis):
        flips.append((axis, flip))
        flip *= 2
    return flips


def halving_sum(buf, names, order):
    for axis, flip in order:
        dim = names.index((axis, flip))
        bit = bit_of(axis, flip)
        keep = lax.dynamic_index_in_dim(buf, bit, axis=dim, keepdims=False)
        send = lax.dynamic_index_in_dim(buf, 1 - bit, axis=dim, keepdims=False)
        buf = keep + exchange(send, axis, flip)
        names = names[:dim] + names[dim + 1 :]
    return buf


def doubling_gather(chunk, order):
    names = []
    for axis, flip in order:
        bit = bit_of(axis, flip)
        got = exchange(chunk, axis, flip)
        low = jnp.where(bit == 0, chunk, got)
        high = jnp.where(bit == 0, got, chunk)
        chunk = jnp.stack([low, high], axis=0)
        names = [(axis, flip)] + names
    return chunk, names


def silu_slope(values):
    sigmoid = jax.nn.sigmoid(values)
    return sigmoid * (1.0 + values * (1.0 - sigmoid))


def contract_rows(left_rows, right_rows):
    return lax.dot_general(
        left_rows, right_rows, (((0,), (0,)), ((), ())), preferred_element_type=jnp.float32
    )


def times_transpose(left_rows, right_cols):
    return lax.dot_general(
        left_rows, right_cols, (((1,), (1,)), ((), ())), preferred_element_type=jnp.float32
    )


def arrange(padded, distant, height, width):
    nearby = [
        padded[:, 1 + row_step : 1 + row_step + height, 1 + col_step : 1 + col_step + width]
        for row_step, col_step in GRID_STEPS
    ]
    return nearby + list(distant)


def validity(height, width, span_rows):
    row_first = lax.axis_index("gx") * height
    col_first = lax.axis_index("gy") * width
    total_rows = height * lax.axis_size("gx")
    total_cols = width * lax.axis_size("gy")
    rows_here = row_first + lax.broadcasted_iota(jnp.int32, (height, width), 0)
    cols_here = col_first + lax.broadcasted_iota(jnp.int32, (height, width), 1)
    masks = []
    for row_step, col_step in GRID_STEPS + [(span_rows, 0), (-span_rows, 0)]:
        inside = (
            (rows_here + row_step >= 0)
            & (rows_here + row_step < total_rows)
            & (cols_here + col_step >= 0)
            & (cols_here + col_step < total_cols)
        )
        masks.append(inside.astype(jnp.float32)[None, :, :, None])
    return masks


def fetch_forward(field, span):
    padded = with_halo(field, (("gx", 1), ("gy", 2)), 1)
    distant = [from_behind(field, "gx", moved_by) for moved_by in (-span, span)]
    return (padded, distant)


def fetch_pair(field, span):
    padded = with_halo(field, (("gx", 1), ("gy", 2)), 1)
    distant = [from_behind(field, "gx", moved_by) for moved_by in (-span, span)]
    return (padded, distant)


def on_device(
    covariance,
    pilot_ids,
    targets,
    encoder_beam_weight,
    norm_gain,
    pilot_table,
    pair_weight,
    edge_bias,
    node_weight,
    node_bias,
    update_weight,
    readout_weight,
):
    samples, height, width = (covariance.shape[0], covariance.shape[1], covariance.shape[2])
    antennas = encoder_beam_weight.shape[0]
    features = encoder_beam_weight.shape[1]
    pilots = pilot_table.shape[0]
    span = lax.axis_size("gx") // 4
    span_rows = span * height
    points = samples * height * width
    total_points = points * lax.axis_size("gx") * lax.axis_size("gy")
    masks = validity(height, width, span_rows)
    degree = masks[0]
    for another in masks[1:]:
        degree = degree + another
    beams = encoder_beam_weight.astype(jnp.float32)
    cov_flat = covariance.reshape(points, antennas * antennas)
    outer = (beams[:, None, :] * beams[None, :, :]).reshape(antennas * antennas, features)
    outer_hi = outer.astype(jnp.bfloat16)
    outer_lo = (outer - outer_hi.astype(jnp.float32)).astype(jnp.bfloat16)
    powers = (
        jnp.dot(cov_flat, outer_hi, preferred_element_type=jnp.float32)
        + jnp.dot(cov_flat, outer_lo, preferred_element_type=jnp.float32)
    ).reshape(samples, height, width, features)
    inverse = lax.rsqrt(jnp.mean(powers * powers, axis=-1, keepdims=True) + EPSILON)
    normed = powers * inverse
    onehot = (pilot_ids.reshape(points, 1) == jnp.arange(pilots, dtype=jnp.int32)[None, :]).astype(
        jnp.float32
    )
    looked = lax.dot_general(
        onehot,
        pilot_table,
        (((1,), (0,)), ((), ())),
        precision=HIGHEST,
        preferred_element_type=jnp.float32,
    )
    hidden = normed * norm_gain + looked.reshape(samples, height, width, features)
    saved = []
    for round_index in range(ROUNDS):
        flat_hidden = hidden.astype(jnp.bfloat16).reshape(points, features)
        pair_proj = jnp.dot(flat_hidden, pair_weight, preferred_element_type=jnp.float32).reshape(
            samples, height, width, 2 * features
        )
        query_part = pair_proj[..., :features].astype(jnp.bfloat16)
        key_part = pair_proj[..., features:].astype(jnp.bfloat16)
        padded, distant = fetch_forward(key_part, span)
        key_near = arrange(padded, distant, height, width)
        query_kept = None
        query_wide = query_part.astype(jnp.float32)
        edge_total = jnp.zeros((samples, height, width, features), jnp.float32)
        for inside, neighbour in zip(masks, key_near):
            edge_total = edge_total + inside * jax.nn.silu(
                query_wide + neighbour.astype(jnp.float32) + edge_bias
            )
        flat_message = (edge_total / degree).astype(jnp.bfloat16).reshape(points, features)
        before = (
            jnp.dot(flat_hidden, node_weight[:features], preferred_element_type=jnp.float32)
            + jnp.dot(flat_message, node_weight[features:], preferred_element_type=jnp.float32)
            + node_bias
        )
        update = jax.nn.silu(before).astype(jnp.bfloat16)
        hidden = hidden + jnp.dot(
            update, update_weight, preferred_element_type=jnp.float32
        ).reshape(samples, height, width, features)
        saved.append(
            (flat_hidden, query_part, key_part, key_near, query_kept, flat_message, before, update)
        )
    final_flat = hidden.astype(jnp.bfloat16).reshape(points, features)
    estimates = times_transpose(readout_weight, final_flat)
    residual_slope = (estimates - targets.reshape(2, points)) * (2.0 / math.sqrt(total_points))
    grad_readout = lax.dot_general(
        residual_slope,
        final_flat.astype(jnp.float32),
        (((1,), (0,)), ((), ())),
        precision=HIGHEST,
        preferred_element_type=jnp.float32,
    )
    readout_wide = readout_weight.astype(jnp.float32)
    grad_hidden = (
        residual_slope[0][:, None] * readout_wide[0][None, :]
        + residual_slope[1][:, None] * readout_wide[1][None, :]
    )
    grad_update = jnp.zeros((features, features), jnp.float32)
    grad_node_bias = jnp.zeros((features,), jnp.float32)
    grad_edge_bias = jnp.zeros((features,), jnp.float32)
    state_list, pair_list, input_list, lower_list = ([], [], [], [])
    for (
        flat_hidden,
        query_part,
        key_part,
        key_near,
        query_kept,
        flat_message,
        before,
        update,
    ) in reversed(saved):
        down_rows = grad_hidden.astype(jnp.bfloat16)
        grad_update = grad_update + contract_rows(update, down_rows)
        grad_before = times_transpose(down_rows, update_weight) * silu_slope(before)
        grad_node_bias = grad_node_bias + jnp.sum(grad_before, axis=0)
        lower_rows = grad_before.astype(jnp.bfloat16)
        grad_inputs = times_transpose(lower_rows, node_weight)
        sending = (
            grad_inputs[:, features:].reshape(samples, height, width, features) / degree
        ).astype(jnp.bfloat16)
        stacked = jnp.concatenate([query_part, sending], axis=-1)
        padded_pair, distant_pair = fetch_pair(stacked, span)
        pair_near = arrange(padded_pair, distant_pair, height, width)
        query_near = [piece_pair[..., :features] for piece_pair in pair_near]
        sending_near = [piece_pair[..., features:] for piece_pair in pair_near]
        sending_wide = sending.astype(jnp.float32)
        query_wide = query_part.astype(jnp.float32)
        key_wide = key_part.astype(jnp.float32)
        grad_query = jnp.zeros((samples, height, width, features), jnp.float32)
        grad_key = jnp.zeros((samples, height, width, features), jnp.float32)
        for inside, key_other, query_other, sending_other in zip(
            masks, key_near, query_near, sending_near
        ):
            grad_query = grad_query + inside * sending_wide * silu_slope(
                query_wide + key_other.astype(jnp.float32) + edge_bias
            )
            grad_key = grad_key + inside * sending_other.astype(jnp.float32) * silu_slope(
                query_other.astype(jnp.float32) + key_wide + edge_bias
            )
        grad_edge_bias = grad_edge_bias + jnp.sum(grad_query, axis=(0, 1, 2))
        pair_rows = (
            jnp.concatenate([grad_query, grad_key], axis=-1)
            .astype(jnp.bfloat16)
            .reshape(points, 2 * features)
        )
        grad_hidden = (
            grad_hidden + grad_inputs[:, :features] + times_transpose(pair_rows, pair_weight)
        )
        state_list.append(flat_hidden)
        pair_list.append(pair_rows)
        input_list.append(jnp.concatenate([flat_hidden, flat_message], axis=1))
        lower_list.append(lower_rows)
    grad_zero = grad_hidden.reshape(samples, height, width, features)
    point_gradient = grad_zero * math.sqrt(total_points)
    grad_gain = jnp.sum(grad_zero * normed, axis=(0, 1, 2))
    grad_table = lax.dot_general(
        onehot,
        grad_hidden,
        (((0,), (0,)), ((), ())),
        precision=HIGHEST,
        preferred_element_type=jnp.float32,
    )
    scaled = grad_zero * norm_gain
    power_gradient = inverse * (scaled - normed * jnp.mean(scaled * normed, axis=-1, keepdims=True))

    power_rows = power_gradient.reshape(points, features)
    power_hi = power_rows.astype(jnp.bfloat16)
    power_lo = (power_rows - power_hi.astype(jnp.float32)).astype(jnp.bfloat16)
    spread = contract_rows(cov_flat, power_hi) + contract_rows(cov_flat, power_lo)
    beam_gradient = jnp.sum(
        spread.reshape(antennas, antennas, features) * beams[None, :, :], axis=1
    )
    rows_state = jnp.concatenate(state_list, axis=0)
    rows_pair = jnp.concatenate(pair_list, axis=0)
    rows_input = jnp.concatenate(input_list, axis=0)
    rows_lower = jnp.concatenate(lower_list, axis=0)
    pair_full = contract_rows(rows_state, rows_pair)
    node_full = contract_rows(rows_input, rows_lower)
    x_flips = flips_of("gx")
    y_flips = flips_of("gy")
    x_count = lax.axis_size("gx")
    y_count = lax.axis_size("gy")
    pieces = x_count * y_count
    replicated = [
        grad_update,
        2.0 * beam_gradient,
        grad_edge_bias,
        grad_node_bias,
        grad_gain,
        grad_table,
        grad_readout,
    ]
    rep_flat = jnp.concatenate([part.reshape(-1) for part in replicated])
    rep_size = rep_flat.shape[0]
    pair_width = pair_full.size // pieces
    node_width = node_full.size // pieces
    rep_piece = -(-(pair_width + node_width + rep_size // pieces + 1) // 1024) * 1024
    rep_piece = rep_piece - pair_width - node_width
    rep_flat = jnp.pad(rep_flat, (0, rep_piece * pieces - rep_size))
    buf = jnp.concatenate(
        [
            pair_full.reshape(pieces, -1),
            node_full.reshape(pieces, -1),
            rep_flat.reshape(pieces, rep_piece),
        ],
        axis=1,
    )
    msb_x = list(reversed(x_flips))
    msb_y = list(reversed(y_flips))
    names = msb_x + msb_y
    buf = buf.reshape([2] * len(names) + [buf.shape[1] // 128, 128])
    chunk = halving_sum(buf, names, y_flips + x_flips)
    gathered, got_names = doubling_gather(chunk, msb_y)
    gathered = jnp.transpose(
        gathered, [got_names.index(name) for name in msb_y] + [len(got_names), len(got_names) + 1]
    ).reshape(y_count, -1)
    grad_pair_weight = gathered[:, :pair_width].reshape(-1, pair_full.shape[1])
    grad_node_weight = gathered[:, pair_width : pair_width + node_width].reshape(
        -1, node_full.shape[1]
    )
    rep_part = gathered[:, pair_width + node_width :]
    rep_all, rep_names = doubling_gather(rep_part, msb_x)
    rep_all = jnp.transpose(
        rep_all, [rep_names.index(name) for name in msb_x] + [len(rep_names), len(rep_names) + 1]
    ).reshape(-1)
    small_sums = []
    offset = 0
    for part in replicated:
        small_sums.append(rep_all[offset : offset + part.size].reshape(part.shape))
        offset += part.size
    return (
        estimates.reshape(2, samples, height, width),
        grad_pair_weight,
        grad_node_weight,
        small_sums[0],
        small_sums[1],
        small_sums[2],
        small_sums[3],
        small_sums[4],
        small_sums[5],
        small_sums[6],
        point_gradient,
    )


def solution(mesh):
    in_specs = (
        P(None, "gx", "gy", None),
        P(None, "gx", "gy"),
        P(None, None, "gx", "gy"),
        P(),
        P(),
        P(),
        P(),
        P(),
        P(),
        P(),
        P(),
        P(),
    )
    out_specs = (
        P(None, None, "gx", "gy"),
        P("gx", None),
        P("gx", None),
        P(),
        P(),
        P(),
        P(),
        P(),
        P(),
        P(),
        P(None, "gx", "gy", None),
    )
    return jax.shard_map(
        on_device, mesh=mesh, in_specs=in_specs, out_specs=out_specs, check_vma=False
    )
```
